32 devices in a mesh: rep: 2 (over y), span: 2 (over x), seq: 4 (over z), head: 2 (over core).
Axes of the slice: x: 2, y: 2, z: 4, core: 2. Of those that a mesh axis runs over, the one named last changes fastest.
Arguments:
- queries: bfloat16 [4, 2, 1024, 4096], P(('rep', 'span'), 'head', None, 'seq'), parts along dimension 0, may hold values from -12 to 12
- keys: bfloat16 [4, 2, 1024, 4096], P(('rep', 'span'), 'head', None, 'seq'), parts along dimension 0, may hold values from -12 to 12
- values: bfloat16 [4, 2, 1024, 4096], P(('rep', 'span'), 'head', None, 'seq'), parts along dimension 0, may hold values from -6 to 6
- span_order: int32 [4], P('rep'), parts along dimension 0, may hold values from 0 to 15, as said below
Outputs:
- attention: bfloat16 [4, 2, 1024, 4096], P(('rep', 'span'), 'head', 'seq'), parts along dimension 0
The draws below stay inside these ranges and needn't reach their ends.
There are 2 independent parts, one for each index of `rep`. The reference program is written for one: setup_inputs(seed, part) draws one part's arguments, and reference() takes and returns one part's arrays. A program takes and returns all parts, laid end to end along the dimension named above; each array names one. Nothing has to cross between parts.
Inputs may be any that keep to these rules, and one draw needn't show every extreme that they name: `span_order`: each group has a different span index.
All inputs are finite; a program needn't handle non-finite values.
Results may differ from the reference program's by a relative error of at most 0.0055.
Values may be sent and summed in bfloat16 or wider, within the bound.
A program may use at most 128 MiB of HBM per device.

```python
import math
import jax
import jax.numpy as jnp
from jax import lax

HD = 128
HALF = 1024
GROUPS = 2
EMBED = 4096
N_HEAD = 2


def pair_draw(key):
    full_shape = (GROUPS, N_HEAD, HALF, EMBED)
    query_key = jax.random.fold_in(key, 11)
    key_key = jax.random.fold_in(key, 12)
    queries = jnp.clip(2.5 * jax.random.normal(query_key, full_shape, jnp.float32), -10.0, 10.0)
    keys = jnp.clip(jax.random.normal(key_key, full_shape, jnp.float32), -4.0, 4.0)
    return (queries, keys)


def draw_queries(key, part):
    return pair_draw(key)[0].astype(jnp.bfloat16)


def draw_keys(key, part):
    return pair_draw(key)[1].astype(jnp.bfloat16)


def draw_span_order(key, part):
    order_key = jax.random.fold_in(key, 21)
    shuffled = jax.random.permutation(order_key, jnp.arange(8 * GROUPS, dtype=jnp.int32))
    return shuffled[:GROUPS].astype(jnp.int32)


def level_of(rng, shape, pieces, smallest, largest):
    factor_of, own = 1.0, jax.random.fold_in(rng, 6)
    for position, shards_of in pieces:
        steps = jnp.exp(jax.random.uniform(jax.random.fold_in(own, position), (shards_of,), jnp.float32, smallest / len(pieces), largest / len(pieces)))
        factor_of = factor_of * jnp.repeat(steps, shape[position] // shards_of).reshape([-1 if axis == position else 1 for axis in range(len(shape))])
    return factor_of


def noise(own_key, shape, deviation, most, pieces=(), held_as=jnp.bfloat16):
    factor_of = level_of(own_key, shape, pieces, -0.22, 0.18) if pieces else 1.0
    entries = jax.random.normal(own_key, shape, jnp.float32) * deviation * factor_of
    return jnp.minimum(jnp.maximum(entries, -most), most).astype(held_as)


def setup_inputs(seed: int = 0, part: int = 0) -> dict:
    splits = jax.random.split(jax.random.key(seed), 5)
    own_keys = jax.random.split(jax.random.fold_in(splits[4], part), 5)
    queries = draw_queries(jax.random.fold_in(jax.random.fold_in(splits[4], part), 71), part)
    keys = draw_keys(jax.random.fold_in(jax.random.fold_in(splits[4], part), 71), part)
    values = noise(own_keys[2], (GROUPS, N_HEAD, HALF, EMBED), 1.0, 6.0, ((0, 2), (1, 2), (3, 4)))
    span_order = draw_span_order(jax.random.fold_in(jax.random.fold_in(splits[4], part), 71), part)
    return {"queries": queries, "keys": keys, "values": values, "span_order": span_order}


def reference(queries, keys, values, span_order):
    group_count = queries.shape[0]
    span_len = queries.shape[1] * queries.shape[2]
    embed_width = queries.shape[3]
    head_count = embed_width // HD
    score_scale = 1.0 / math.sqrt(HD)
    bias_rate = 1.0 / (2.0 * group_count)
    key_heads = keys.reshape(group_count * span_len, head_count, HD).transpose(1, 0, 2)
    value_heads = values.reshape(group_count * span_len, head_count, HD).transpose(1, 0, 2)
    key_spans = jnp.repeat(span_order, span_len)
    results = []
    for group in range(group_count):
        allowed = key_spans <= span_order[group]
        distance_bias = (span_order[group] - key_spans).astype(jnp.float32) * jnp.float32(bias_rate)

        def one_head(inputs):
            query_head, key_head, value_head = inputs
            scores = jnp.dot(query_head.astype(jnp.float32), key_head.astype(jnp.float32).T) * score_scale
            scores = scores - distance_bias[None, :]
            scores = jnp.where(allowed[None, :], scores, jnp.float32(-1e+30))
            row_max = lax.optimization_barrier(jnp.max(scores, axis=1, keepdims=True))
            weights = jnp.where(allowed[None, :], jnp.exp(scores - row_max), 0.0).astype(jnp.bfloat16)
            totals = lax.optimization_barrier(jnp.sum(weights.astype(jnp.float32), axis=1, keepdims=True))
            weighted = jnp.dot(weights.astype(jnp.float32), value_head.astype(jnp.float32))
            return (weighted / totals).astype(jnp.bfloat16)
        query_heads = queries[group].reshape(span_len, head_count, HD).transpose(1, 0, 2)
        result = lax.map(one_head, (query_heads, key_heads, value_heads))
        results.append(result.transpose(1, 0, 2).reshape(queries.shape[1], queries.shape[2], embed_width))
    return jnp.stack(results)
```

```python
import functools
import math

import jax
import jax.numpy as jnp
from jax import lax
from jax.experimental import pallas as pl
from jax.experimental.pallas import tpu as pltpu
from jax.sharding import PartitionSpec as P

HD = 128


def lookup(span_order, block_index):
    table = jnp.arange(span_order.shape[0], dtype=jnp.int32)
    return jnp.sum(
        jnp.where(block_index[:, None] == table[None, :], span_order[None, :], 0), axis=1
    )


def initial(query_heads):
    query_count = query_heads.shape[0]
    local_heads = query_heads.shape[1]
    return (
        jnp.full((local_heads, query_count), -1e30, jnp.float32),
        jnp.zeros((local_heads, query_count), jnp.float32),
        jnp.zeros((local_heads, query_count, HD), jnp.float32),
    )


def attend(running, query_heads, key_piece, value_piece, block_span, own_span, bias_rate):
    block_count = key_piece.shape[0]
    piece_rows = key_piece.shape[1]
    local_heads = key_piece.shape[2] // HD
    key_count = block_count * piece_rows
    score_scale = 1.0 / math.sqrt(HD)
    key_spans = jnp.repeat(block_span, piece_rows)
    allowed = key_spans <= own_span
    distance_bias = (own_span - key_spans).astype(jnp.float32) * jnp.float32(bias_rate)
    block_size = 1024
    block_total = key_count // block_size
    key_blocks = key_piece.reshape(block_total, block_size, local_heads, HD)
    value_blocks = value_piece.reshape(block_total, block_size, local_heads, HD)
    allow_blocks = allowed.reshape(block_total, block_size)
    bias_blocks = distance_bias.reshape(block_total, block_size)

    def advance(status, block_item):
        key_block, value_block, allow_block, bias_block = block_item
        maxima, totals, weighted = status
        scores = (
            jnp.einsum("qhd,khd->hqk", query_heads, key_block, preferred_element_type=jnp.float32)
            * score_scale
        )
        scores = scores - bias_block[None, None, :]
        scores = jnp.where(allow_block[None, None, :], scores, jnp.float32(-1e30))
        new_max = jnp.maximum(maxima, jnp.max(scores, axis=2))
        weights = jnp.where(
            allow_block[None, None, :], jnp.exp(scores - new_max[:, :, None]), 0.0
        ).astype(jnp.bfloat16)
        shrink = jnp.exp(maxima - new_max)
        totals = totals * shrink + jnp.sum(weights.astype(jnp.float32), axis=2)
        weighted = weighted * shrink[:, :, None] + jnp.einsum(
            "hqk,khd->hqd", weights, value_block, preferred_element_type=jnp.float32
        )
        return ((new_max, totals, weighted), None)

    running, unused = lax.scan(
        advance, running, (key_blocks, value_blocks, allow_blocks, bias_blocks)
    )
    return running


def finish(running):
    maxima, totals, weighted = running
    local_heads = weighted.shape[0]
    query_count = weighted.shape[1]
    output = (weighted / totals[:, :, None]).transpose(1, 0, 2)
    return output.reshape(1, 1, query_count, local_heads * HD).astype(jnp.bfloat16)


def per_device_general(queries, keys, values, span_order):
    half_rows = queries.shape[2]
    local_width = queries.shape[3]
    local_heads = local_width // HD
    halves = lax.axis_size("head")
    bias_rate = 1.0 / (2.0 * span_order.shape[0])
    own_span = lookup(span_order, jnp.reshape(lax.axis_index("span"), (1,)))[0]
    query_heads = queries.reshape(half_rows, local_heads, HD)
    pieces = (
        lax.all_gather(keys, ("span", "head"), axis=0, tiled=True),
        lax.all_gather(values, ("span", "head"), axis=0, tiled=True),
    )
    count = pieces[0].shape[0]
    block_index = jnp.arange(count, dtype=jnp.int32) // halves
    key_piece = pieces[0].reshape(count, half_rows, local_width)
    value_piece = pieces[1].reshape(count, half_rows, local_width)
    running = attend(
        initial(query_heads),
        query_heads,
        key_piece,
        value_piece,
        lookup(span_order, block_index),
        own_span,
        bias_rate,
    )
    result = finish(running)
    return lax.all_to_all(result, "seq", split_axis=2, concat_axis=3, tiled=True)


MESH = pl.DeviceIdType.MESH
ROWS = 256
LOG2E = 1.4426950408889634


def fused_kernel(
    heads, seq_count, shift_ref, q_ref, k_ref, v_ref, out_ref,
    kp, vp, kx, vx, kd, vd, stage,
    p_send, p_recv, x_send, x_recv, d_send, d_recv, z_send, z_recv, own_sem,
):
    rep, span = lax.axis_index("rep"), lax.axis_index("span")
    seq, core = lax.axis_index("seq"), lax.axis_index("head")
    partner = (rep, span, seq, 1 - core)
    across = (rep, 1 - span, seq, core)
    tokens, width = q_ref.shape
    part = tokens // seq_count

    def along(step):
        return lax.rem(seq + step, seq_count)

    barrier = pltpu.get_barrier_semaphore()
    peers = [partner, across] + [(rep, span, along(i), core) for i in range(1, seq_count)]
    for peer in peers:
        pl.semaphore_signal(barrier, inc=1, device_id=peer, device_id_type=MESH)
    pl.semaphore_wait(barrier, len(peers))

    def cols(h):
        return pl.ds(pl.multiple_of(h * HD, HD), HD)

    def move(src, dst, send, recv, which, h, device):
        return pltpu.make_async_remote_copy(
            src_ref=src.at[:, cols(h)],
            dst_ref=dst.at[:, cols(h)],
            send_sem=send.at[which, h],
            recv_sem=recv.at[which, h],
            device_id=device,
            device_id_type=MESH,
        )

    def to_across(h):
        return (
            move(k_ref, kx, x_send, x_recv, 0, h, across),
            move(v_ref, vx, x_send, x_recv, 1, h, across),
        )

    def to_partner(h):
        return (
            move(k_ref, kp, p_send, p_recv, 0, h, partner),
            move(v_ref, vp, p_send, p_recv, 1, h, partner),
        )

    def relay(h):
        return (
            move(kx, kd, d_send, d_recv, 0, h, partner),
            move(vx, vd, d_send, d_recv, 1, h, partner),
        )

    def out_cols(from_seq, h):
        return pl.ds(pl.multiple_of(from_seq * width + h * HD, HD), HD)

    def to_seq(h, step):
        target = along(step)
        return pltpu.make_async_remote_copy(
            src_ref=stage.at[pl.ds(pl.multiple_of(target * part, part), part), cols(h)],
            dst_ref=out_ref.at[:, out_cols(seq, h)],
            send_sem=z_send.at[step - 1, h],
            recv_sem=z_recv.at[step - 1, h],
            device_id=(rep, span, target, core),
            device_id_type=MESH,
        )

    def to_self(h):
        return pltpu.make_async_copy(
            stage.at[pl.ds(pl.multiple_of(seq * part, part), part), cols(h)],
            out_ref.at[:, out_cols(seq, h)],
            own_sem.at[h],
        )

    def launch(h, carry):
        for copy in to_across(h) + to_partner(h):
            copy.start()
        return carry

    lax.fori_loop(0, heads, launch, 0)

    rate = jnp.float32(LOG2E / math.sqrt(HD))
    shift = shift_ref[0]

    def one_head(h, carry):
        for copy in to_across(h):
            copy.wait_recv()
        for copy in relay(h):
            copy.start()
        for copy in to_partner(h):
            copy.wait_recv()
        for copy in relay(h):
            copy.wait_recv()

        def tile(t, inner):
            rows = pl.ds(pl.multiple_of(t * ROWS, ROWS), ROWS)
            query = q_ref[rows, cols(h)]

            def score(ref):
                return lax.dot_general(
                    query, ref[:, cols(h)], (((1,), (1,)), ((), ())),
                    preferred_element_type=jnp.float32,
                )

            near = [score(k_ref), score(kp)]
            far = [score(kx), score(kd)]
            near_max = jnp.max(jnp.maximum(near[0], near[1]), axis=1, keepdims=True) * rate
            far_max = jnp.max(jnp.maximum(far[0], far[1]), axis=1, keepdims=True) * rate
            top = jnp.maximum(near_max, far_max - shift)
            far_top = top + shift
            total = None
            ones = jnp.ones((tokens, HD), jnp.bfloat16)
            for scores, offset, ref in (
                (near[0], top, v_ref), (near[1], top, vp),
                (far[0], far_top, vx), (far[1], far_top, vd),
            ):
                weights = jnp.exp2(scores * rate - offset).astype(jnp.bfloat16)
                value = jnp.concatenate([ref[:, cols(h)], ones], axis=1)
                term = jnp.dot(weights, value, preferred_element_type=jnp.float32)
                total = term if total is None else total + term
            stage[rows, cols(h)] = (total[:, :HD] / total[:, HD:]).astype(jnp.bfloat16)
            return inner

        lax.fori_loop(0, tokens // ROWS, tile, 0)
        for step in range(1, seq_count):
            to_seq(h, step).start()
        to_self(h).start()
        return carry

    lax.fori_loop(0, heads, one_head, 0)

    def drain(h, carry):
        for copy in to_across(h) + to_partner(h) + relay(h):
            copy.wait_send()
        for step in range(1, seq_count):
            to_seq(h, step).wait_send()
            to_seq(h, step).wait_recv()
        to_self(h).wait()
        return carry

    lax.fori_loop(0, heads, drain, 0)


def per_device_fused(queries, keys, values, span_order):
    tokens, width = queries.shape[2], queries.shape[3]
    heads = width // HD
    seq_count = lax.axis_size("seq")
    bias_rate = 1.0 / (2.0 * span_order.shape[0])
    span = lax.axis_index("span")
    own = lookup(span_order, jnp.reshape(span, (1,)))
    other = lookup(span_order, jnp.reshape(1 - span, (1,)))
    bias = (own - other).astype(jnp.float32) * jnp.float32(bias_rate)
    shift = jnp.where(other <= own, bias * jnp.float32(LOG2E), jnp.float32(1e30))
    whole = pl.BlockSpec(memory_space=pltpu.VMEM)
    block = pltpu.VMEM((tokens, width), jnp.bfloat16)
    pairs = pltpu.SemaphoreType.DMA((2, heads))
    lines = pltpu.SemaphoreType.DMA((seq_count - 1, heads))
    result = pl.pallas_call(
        functools.partial(fused_kernel, heads, seq_count),
        out_shape=jax.ShapeDtypeStruct((tokens // seq_count, width * seq_count), jnp.bfloat16),
        in_specs=[pl.BlockSpec(memory_space=pltpu.SMEM), whole, whole, whole],
        out_specs=whole,
        scratch_shapes=[block] * 7 + [pairs] * 6 + [lines] * 2 + [pltpu.SemaphoreType.DMA((heads,))],
        compiler_params=pltpu.CompilerParams(
            collective_id=0, has_side_effects=True, vmem_limit_bytes=60 * 1024 * 1024
        ),
    )(
        shift,
        queries.reshape(tokens, width),
        keys.reshape(tokens, width),
        values.reshape(tokens, width),
    )
    return result.reshape(1, 1, tokens // seq_count, width * seq_count)


def per_device(queries, keys, values, span_order):
    tokens = queries.shape[2]
    seq_count = lax.axis_size("seq")
    part = tokens // seq_count
    fits = (
        lax.axis_size("span") == 2
        and lax.axis_size("head") == 2
        and tokens % ROWS == 0
        and part % 16 == 0
        and seq_count <= 8
    )
    run = per_device_fused if fits else per_device_general
    return run(queries, keys, values, span_order)


def solution(mesh):
    return jax.shard_map(
        per_device,
        mesh=mesh,
        in_specs=(
            P(("rep", "span"), "head", None, "seq"),
            P(("rep", "span"), "head", None, "seq"),
            P(("rep", "span"), "head", None, "seq"),
            P("rep"),
        ),
        out_specs=P(("rep", "span"), "head", "seq", None),
        check_vma=False,
    )
```

```python
import functools
import math

import jax
import jax.numpy as jnp
from jax import lax
from jax.experimental import pallas as pl
from jax.experimental.pallas import tpu as pltpu
from jax.sharding import PartitionSpec as P

HD = 128


def lookup(span_order, block_index):
    table = jnp.arange(span_order.shape[0], dtype=jnp.int32)
    return jnp.sum(
        jnp.where(block_index[:, None] == table[None, :], span_order[None, :], 0), axis=1
    )


def initial(query_heads):
    query_count = query_heads.shape[0]
    local_heads = query_heads.shape[1]
    return (
        jnp.full((local_heads, query_count), -1e30, jnp.float32),
        jnp.zeros((local_heads, query_count), jnp.float32),
        jnp.zeros((local_heads, query_count, HD), jnp.float32),
    )


def attend(running, query_heads, key_piece, value_piece, block_span, own_span, bias_rate):
    block_count = key_piece.shape[0]
    piece_rows = key_piece.shape[1]
    local_heads = key_piece.shape[2] // HD
    key_count = block_count * piece_rows
    score_scale = 1.0 / math.sqrt(HD)
    key_spans = jnp.repeat(block_span, piece_rows)
    allowed = key_spans <= own_span
    distance_bias = (own_span - key_spans).astype(jnp.float32) * jnp.float32(bias_rate)
    block_size = 1024
    block_total = key_count // block_size
    key_blocks = key_piece.reshape(block_total, block_size, local_heads, HD)
    value_blocks = value_piece.reshape(block_total, block_size, local_heads, HD)
    allow_blocks = allowed.reshape(block_total, block_size)
    bias_blocks = distance_bias.reshape(block_total, block_size)

    def advance(status, block_item):
        key_block, value_block, allow_block, bias_block = block_item
        maxima, totals, weighted = status
        scores = (
            jnp.einsum("qhd,khd->hqk", query_heads, key_block, preferred_element_type=jnp.float32)
            * score_scale
        )
        scores = scores - bias_block[None, None, :]
        scores = jnp.where(allow_block[None, None, :], scores, jnp.float32(-1e30))
        new_max = jnp.maximum(maxima, jnp.max(scores, axis=2))
        weights = jnp.where(
            allow_block[None, None, :], jnp.exp(scores - new_max[:, :, None]), 0.0
        ).astype(jnp.bfloat16)
        shrink = jnp.exp(maxima - new_max)
        totals = totals * shrink + jnp.sum(weights.astype(jnp.float32), axis=2)
        weighted = weighted * shrink[:, :, None] + jnp.einsum(
            "hqk,khd->hqd", weights, value_block, preferred_element_type=jnp.float32
        )
        return ((new_max, totals, weighted), None)

    running, unused = lax.scan(
        advance, running, (key_blocks, value_blocks, allow_blocks, bias_blocks)
    )
    return running


def finish(running):
    maxima, totals, weighted = running
    local_heads = weighted.shape[0]
    query_count = weighted.shape[1]
    output = (weighted / totals[:, :, None]).transpose(1, 0, 2)
    return output.reshape(1, 1, query_count, local_heads * HD).astype(jnp.bfloat16)


def per_device_general(queries, keys, values, span_order):
    half_rows = queries.shape[2]
    local_width = queries.shape[3]
    local_heads = local_width // HD
    halves = lax.axis_size("head")
    bias_rate = 1.0 / (2.0 * span_order.shape[0])
    own_span = lookup(span_order, jnp.reshape(lax.axis_index("span"), (1,)))[0]
    query_heads = queries.reshape(half_rows, local_heads, HD)
    pieces = (
        lax.all_gather(keys, ("span", "head"), axis=0, tiled=True),
        lax.all_gather(values, ("span", "head"), axis=0, tiled=True),
    )
    count = pieces[0].shape[0]
    block_index = jnp.arange(count, dtype=jnp.int32) // halves
    key_piece = pieces[0].reshape(count, half_rows, local_width)
    value_piece = pieces[1].reshape(count, half_rows, local_width)
    running = attend(
        initial(query_heads),
        query_heads,
        key_piece,
        value_piece,
        lookup(span_order, block_index),
        own_span,
        bias_rate,
    )
    result = finish(running)
    return lax.all_to_all(result, "seq", split_axis=2, concat_axis=3, tiled=True)


MESH = pl.DeviceIdType.MESH
ROWS = 256
LOG2E = 1.4426950408889634
RATE = LOG2E / math.sqrt(HD)


def fused_kernel(
    heads, seq_count, scalars_ref, q_ref, k_ref, v_ref, pay_ref, out_ref,
    kp, vp, px, pd, own, own_lse, cross, cross_lse, back, back_lse, stage, jq, jk, jv,
    p_send, p_recv, x_send, x_recv, d_send, d_recv, r_send, r_recv, z_send, z_recv, own_sem,
):
    rep, span = lax.axis_index("rep"), lax.axis_index("span")
    seq, core = lax.axis_index("seq"), lax.axis_index("head")
    partner = (rep, span, seq, 1 - core)
    across = (rep, 1 - span, seq, core)
    tokens, width = q_ref.shape
    part = tokens // seq_count
    jobs = heads // 2

    def along(step):
        return lax.rem(seq + step, seq_count)

    barrier = pltpu.get_barrier_semaphore()
    peers = [partner, across] + [(rep, span, along(i), core) for i in range(1, seq_count)]
    for peer in peers:
        pl.semaphore_signal(barrier, inc=1, device_id=peer, device_id_type=MESH)
    pl.semaphore_wait(barrier, len(peers))

    def cols(h):
        return pl.ds(pl.multiple_of(h * HD, HD), HD)

    def head_of(n):
        return lax.rem(n, 2) * jobs + n // 2

    def move(src, dst, send, recv, which, h, column, device):
        return pltpu.make_async_remote_copy(
            src_ref=src.at[:, cols(column)],
            dst_ref=dst.at[:, cols(column)],
            send_sem=send.at[which, h],
            recv_sem=recv.at[which, h],
            device_id=device,
            device_id_type=MESH,
        )

    def to_partner(h):
        return (
            move(k_ref, kp, p_send, p_recv, 0, h, h, partner),
            move(v_ref, vp, p_send, p_recv, 1, h, h, partner),
        )

    def to_across(j):
        return (
            move(pay_ref, px, x_send, x_recv, 0, j, j, across),
            move(pay_ref, px, x_send, x_recv, 1, j, j + jobs, across),
        )

    def relay(j):
        return (
            move(px, pd, d_send, d_recv, 0, j, j, partner),
            move(px, pd, d_send, d_recv, 1, j, j + jobs, partner),
        )

    def give_back(j):
        return (
            move(cross, back, r_send, r_recv, 0, j, j, across),
            pltpu.make_async_remote_copy(
                src_ref=cross_lse.at[j],
                dst_ref=back_lse.at[j],
                send_sem=r_send.at[1, j],
                recv_sem=r_recv.at[1, j],
                device_id=across,
                device_id_type=MESH,
            ),
        )

    def out_cols(from_seq, h):
        return pl.ds(pl.multiple_of(from_seq * width + h * HD, HD), HD)

    def to_seq(h, step):
        target = along(step)
        return pltpu.make_async_remote_copy(
            src_ref=stage.at[pl.ds(pl.multiple_of(target * part, part), part), cols(h)],
            dst_ref=out_ref.at[:, out_cols(seq, h)],
            send_sem=z_send.at[step - 1, h],
            recv_sem=z_recv.at[step - 1, h],
            device_id=(rep, span, target, core),
            device_id_type=MESH,
        )

    def to_self(h):
        return pltpu.make_async_copy(
            stage.at[pl.ds(pl.multiple_of(seq * part, part), part), cols(h)],
            out_ref.at[:, out_cols(seq, h)],
            own_sem.at[h],
        )

    def spread(h):
        for step in range(1, seq_count):
            to_seq(h, step).start()
        to_self(h).start()

    def launch(n, carry):
        for copy in to_partner(head_of(n)):
            copy.start()
        return carry

    def launch_across(j, carry):
        for copy in to_across(j):
            copy.start()
        return carry

    lax.fori_loop(0, jobs, launch_across, 0)
    lax.fori_loop(0, heads, launch, 0)

    shift = scalars_ref[0]
    higher = scalars_ref[1]
    rate = jnp.float32(RATE)

    def attend_rows(query, key_blocks, value_blocks):
        scores = [
            lax.dot_general(
                query, key, (((1,), (1,)), ((), ())), preferred_element_type=jnp.float32
            )
            for key in key_blocks
        ]
        top = jnp.max(jnp.maximum(scores[0], scores[1]), axis=1, keepdims=True) * rate
        ones = jnp.ones((tokens, HD), jnp.bfloat16)
        total = None
        for score, value in zip(scores, value_blocks):
            weights = jnp.exp2(score * rate - top).astype(jnp.bfloat16)
            term = jnp.dot(
                weights, jnp.concatenate([value, ones], axis=1),
                preferred_element_type=jnp.float32,
            )
            total = term if total is None else total + term
        sums = total[:, HD:]
        return total[:, :HD] / sums, top + jnp.log(sums) * jnp.float32(LOG2E)

    def merge(near, near_lse, far, far_lse):
        far_lse = far_lse - shift
        top = jnp.maximum(near_lse, far_lse)
        near_part, far_part = jnp.exp2(near_lse - top), jnp.exp2(far_lse - top)
        mixed = (near * near_part + far * far_part) / (near_part + far_part)
        return mixed.astype(jnp.bfloat16)

    def choose(first, second):
        picked = first.astype(jnp.float32) * higher + second.astype(jnp.float32) * (1.0 - higher)
        return picked.astype(jnp.bfloat16)

    def step(n, carry):
        @pl.when(n < heads)
        def own_job():
            h = head_of(n)
            for copy in to_partner(h):
                copy.wait_recv()
            for t in range(tokens // ROWS):
                rows = pl.ds(t * ROWS, ROWS)
                result, lse = attend_rows(
                    q_ref[rows, cols(h)],
                    (k_ref[:, cols(h)], kp[:, cols(h)]),
                    (v_ref[:, cols(h)], vp[:, cols(h)]),
                )
                own[rows, cols(h)] = result
                own_lse[rows, cols(h)] = lse

        @pl.when(lax.rem(n, 2) == 1)
        def pass_on():
            j = n // 2
            for copy in to_across(j):
                copy.wait_recv()
            for copy in relay(j):
                copy.start()

        @pl.when(jnp.logical_and(lax.rem(n, 2) == 0, n > 0))
        def cross_job():
            j = n // 2 - 1
            b = j + jobs
            for copy in relay(j):
                copy.wait_recv()
            jq[...] = choose(q_ref[:, cols(j)], px[:, cols(j)])
            jk[0] = choose(px[:, cols(j)], k_ref[:, cols(b)])
            jk[1] = choose(pd[:, cols(j)], kp[:, cols(b)])
            jv[0] = choose(px[:, cols(b)], v_ref[:, cols(b)])
            jv[1] = choose(pd[:, cols(b)], vp[:, cols(b)])
            for t in range(tokens // ROWS):
                rows = pl.ds(t * ROWS, ROWS)
                result, lse = attend_rows(jq[rows, :], (jk[0], jk[1]), (jv[0], jv[1]))
                cross[rows, cols(j)] = result.astype(jnp.bfloat16)
                cross_lse[j, :, rows] = lse.T[:8, :]
                stage[rows, cols(j)] = merge(
                    own[rows, cols(j)], own_lse[rows, cols(j)], result, lse
                )
            for copy in give_back(j):
                copy.start()
            spread(j)

        return carry

    lax.fori_loop(0, heads + 1, step, 0)

    def complete(j, carry):
        b = j + jobs
        for copy in give_back(j):
            copy.wait_recv()
        for t in range(tokens // ROWS):
            rows = pl.ds(t * ROWS, ROWS)
            lse = jnp.broadcast_to(back_lse[j, 0:1, rows], (HD, ROWS)).T
            stage[rows, cols(b)] = merge(
                own[rows, cols(b)], own_lse[rows, cols(b)],
                back[rows, cols(j)].astype(jnp.float32), lse,
            )
        spread(b)
        return carry

    lax.fori_loop(0, jobs, complete, 0)

    def drain(h, carry):
        for copy in to_partner(h):
            copy.wait_send()
        for hop in range(1, seq_count):
            to_seq(h, hop).wait_send()
            to_seq(h, hop).wait_recv()
        to_self(h).wait()
        return carry

    def drain_jobs(j, carry):
        for copy in to_across(j) + relay(j) + give_back(j):
            copy.wait_send()
        return carry

    lax.fori_loop(0, jobs, drain_jobs, 0)
    lax.fori_loop(0, heads, drain, 0)


def per_device_fused(queries, keys, values, span_order):
    tokens, width = queries.shape[2], queries.shape[3]
    heads = width // HD
    jobs = heads // 2
    half = jobs * HD
    seq_count = lax.axis_size("seq")
    bias_rate = 1.0 / (2.0 * span_order.shape[0])
    span = lax.axis_index("span")
    own = lookup(span_order, jnp.reshape(span, (1,)))
    other = lookup(span_order, jnp.reshape(1 - span, (1,)))
    bias = (own - other).astype(jnp.float32) * jnp.float32(bias_rate)
    higher = other <= own
    shift = jnp.where(higher, bias * jnp.float32(LOG2E), jnp.float32(1e30))
    scalars = jnp.concatenate([shift, higher.astype(jnp.float32)])
    query, key, value = (a.reshape(tokens, width) for a in (queries, keys, values))
    payload = jnp.where(
        higher[0],
        jnp.concatenate([query[:, half:], query[:, :half]], axis=1),
        jnp.concatenate([key[:, :half], value[:, :half]], axis=1),
    )
    whole = pl.BlockSpec(memory_space=pltpu.VMEM)
    block = pltpu.VMEM((tokens, width), jnp.bfloat16)
    wide = pltpu.VMEM((tokens, width), jnp.float32)
    narrow = pltpu.VMEM((tokens, half), jnp.bfloat16)
    rows = pltpu.VMEM((jobs, 8, tokens), jnp.float32)
    both = pltpu.VMEM((2, tokens, HD), jnp.bfloat16)
    pairs = pltpu.SemaphoreType.DMA((2, heads))
    few = pltpu.SemaphoreType.DMA((2, jobs))
    lines = pltpu.SemaphoreType.DMA((seq_count - 1, heads))
    result = pl.pallas_call(
        functools.partial(fused_kernel, heads, seq_count),
        out_shape=jax.ShapeDtypeStruct((tokens // seq_count, width * seq_count), jnp.bfloat16),
        in_specs=[pl.BlockSpec(memory_space=pltpu.SMEM), whole, whole, whole, whole],
        out_specs=whole,
        scratch_shapes=[block] * 4
        + [wide] * 2
        + [narrow, rows, narrow, rows, block]
        + [pltpu.VMEM((tokens, HD), jnp.bfloat16), both, both]
        + [pairs] * 2
        + [few] * 6
        + [lines] * 2
        + [pltpu.SemaphoreType.DMA((heads,))],
        compiler_params=pltpu.CompilerParams(
            collective_id=0, has_side_effects=True, vmem_limit_bytes=60 * 1024 * 1024
        ),
    )(scalars, query, key, value, payload)
    return result.reshape(1, 1, tokens // seq_count, width * seq_count)


def per_device(queries, keys, values, span_order):
    tokens = queries.shape[2]
    seq_count = lax.axis_size("seq")
    part = tokens // seq_count
    fits = (
        lax.axis_size("span") == 2
        and lax.axis_size("head") == 2
        and tokens % ROWS == 0
        and part % 16 == 0
        and queries.shape[3] % (2 * HD) == 0
        and seq_count <= 8
    )
    run = per_device_fused if fits else per_device_general
    return run(queries, keys, values, span_order)


def solution(mesh):
    return jax.shard_map(
        per_device,
        mesh=mesh,
        in_specs=(
            P(("rep", "span"), "head", None, "seq"),
            P(("rep", "span"), "head", None, "seq"),
            P(("rep", "span"), "head", None, "seq"),
            P("rep"),
        ),
        out_specs=P(("rep", "span"), "head", "seq", None),
        check_vma=False,
    )
```

```python
import functools
import math

import jax
import jax.numpy as jnp
from jax import lax
from jax.experimental import pallas as pl
from jax.experimental.pallas import tpu as pltpu
from jax.sharding import PartitionSpec as P

HD = 128


def lookup(span_order, block_index):
    table = jnp.arange(span_order.shape[0], dtype=jnp.int32)
    return jnp.sum(
        jnp.where(block_index[:, None] == table[None, :], span_order[None, :], 0), axis=1
    )


def initial(query_heads):
    query_count = query_heads.shape[0]
    local_heads = query_heads.shape[1]
    return (
        jnp.full((local_heads, query_count), -1e30, jnp.float32),
        jnp.zeros((local_heads, query_count), jnp.float32),
        jnp.zeros((local_heads, query_count, HD), jnp.float32),
    )


def attend(running, query_heads, key_piece, value_piece, block_span, own_span, bias_rate):
    block_count = key_piece.shape[0]
    piece_rows = key_piece.shape[1]
    local_heads = key_piece.shape[2] // HD
    key_count = block_count * piece_rows
    score_scale = 1.0 / math.sqrt(HD)
    key_spans = jnp.repeat(block_span, piece_rows)
    allowed = key_spans <= own_span
    distance_bias = (own_span - key_spans).astype(jnp.float32) * jnp.float32(bias_rate)
    block_size = 1024
    block_total = key_count // block_size
    key_blocks = key_piece.reshape(block_total, block_size, local_heads, HD)
    value_blocks = value_piece.reshape(block_total, block_size, local_heads, HD)
    allow_blocks = allowed.reshape(block_total, block_size)
    bias_blocks = distance_bias.reshape(block_total, block_size)

    def advance(status, block_item):
        key_block, value_block, allow_block, bias_block = block_item
        maxima, totals, weighted = status
        scores = (
            jnp.einsum("qhd,khd->hqk", query_heads, key_block, preferred_element_type=jnp.float32)
            * score_scale
        )
        scores = scores - bias_block[None, None, :]
        scores = jnp.where(allow_block[None, None, :], scores, jnp.float32(-1e30))
        new_max = jnp.maximum(maxima, jnp.max(scores, axis=2))
        weights = jnp.where(
            allow_block[None, None, :], jnp.exp(scores - new_max[:, :, None]), 0.0
        ).astype(jnp.bfloat16)
        shrink = jnp.exp(maxima - new_max)
        totals = totals * shrink + jnp.sum(weights.astype(jnp.float32), axis=2)
        weighted = weighted * shrink[:, :, None] + jnp.einsum(
            "hqk,khd->hqd", weights, value_block, preferred_element_type=jnp.float32
        )
        return ((new_max, totals, weighted), None)

    running, unused = lax.scan(
        advance, running, (key_blocks, value_blocks, allow_blocks, bias_blocks)
    )
    return running


def finish(running):
    maxima, totals, weighted = running
    local_heads = weighted.shape[0]
    query_count = weighted.shape[1]
    output = (weighted / totals[:, :, None]).transpose(1, 0, 2)
    return output.reshape(1, 1, query_count, local_heads * HD).astype(jnp.bfloat16)


def per_device_general(queries, keys, values, span_order):
    half_rows = queries.shape[2]
    local_width = queries.shape[3]
    local_heads = local_width // HD
    halves = lax.axis_size("head")
    bias_rate = 1.0 / (2.0 * span_order.shape[0])
    own_span = lookup(span_order, jnp.reshape(lax.axis_index("span"), (1,)))[0]
    query_heads = queries.reshape(half_rows, local_heads, HD)
    pieces = (
        lax.all_gather(keys, ("span", "head"), axis=0, tiled=True),
        lax.all_gather(values, ("span", "head"), axis=0, tiled=True),
    )
    count = pieces[0].shape[0]
    block_index = jnp.arange(count, dtype=jnp.int32) // halves
    key_piece = pieces[0].reshape(count, half_rows, local_width)
    value_piece = pieces[1].reshape(count, half_rows, local_width)
    running = attend(
        initial(query_heads),
        query_heads,
        key_piece,
        value_piece,
        lookup(span_order, block_index),
        own_span,
        bias_rate,
    )
    result = finish(running)
    return lax.all_to_all(result, "seq", split_axis=2, concat_axis=3, tiled=True)


MESH = pl.DeviceIdType.MESH
ROWS = 256
LOG2E = 1.4426950408889634
RATE = LOG2E / math.sqrt(HD)


def fused_kernel(
    heads, seq_count, scalars_ref, q_ref, k_ref, v_ref, out_ref,
    kp, vp, px, pd, own, own_lse, cross, cross_lse, back, back_lse, stage, jq, jk, jv, pay_ref,
    p_send, p_recv, x_send, x_recv, d_send, d_recv, r_send, r_recv, z_send, z_recv, own_sem,
):
    rep, span = lax.axis_index("rep"), lax.axis_index("span")
    seq, core = lax.axis_index("seq"), lax.axis_index("head")
    partner = (rep, span, seq, 1 - core)
    across = (rep, 1 - span, seq, core)
    tokens, width = q_ref.shape
    part = tokens // seq_count
    jobs = heads // 2

    def along(step):
        return lax.rem(seq + step, seq_count)

    barrier = pltpu.get_barrier_semaphore()
    peers = [partner, across] + [(rep, span, along(i), core) for i in range(1, seq_count)]
    for peer in peers:
        pl.semaphore_signal(barrier, inc=1, device_id=peer, device_id_type=MESH)
    pl.semaphore_wait(barrier, len(peers))

    def cols(h):
        return pl.ds(pl.multiple_of(h * HD, HD), HD)

    def head_of(n):
        return lax.rem(n, 2) * jobs + n // 2

    def move(src, dst, send, recv, which, h, column, device):
        return pltpu.make_async_remote_copy(
            src_ref=src.at[:, cols(column)],
            dst_ref=dst.at[:, cols(column)],
            send_sem=send.at[which, h],
            recv_sem=recv.at[which, h],
            device_id=device,
            device_id_type=MESH,
        )

    def to_partner(h):
        return (
            move(k_ref, kp, p_send, p_recv, 0, h, h, partner),
            move(v_ref, vp, p_send, p_recv, 1, h, h, partner),
        )

    def to_across(j):
        return (
            move(pay_ref, px, x_send, x_recv, 0, j, j, across),
            move(pay_ref, px, x_send, x_recv, 1, j, j + jobs, across),
        )

    def relay(j):
        return (
            move(px, pd, d_send, d_recv, 0, j, j, partner),
            move(px, pd, d_send, d_recv, 1, j, j + jobs, partner),
        )

    def give_back(j):
        return (
            move(cross, back, r_send, r_recv, 0, j, j, across),
            pltpu.make_async_remote_copy(
                src_ref=cross_lse.at[j],
                dst_ref=back_lse.at[j],
                send_sem=r_send.at[1, j],
                recv_sem=r_recv.at[1, j],
                device_id=across,
                device_id_type=MESH,
            ),
        )

    def out_cols(from_seq, h):
        return pl.ds(pl.multiple_of(from_seq * width + h * HD, HD), HD)

    def to_seq(h, step):
        target = along(step)
        return pltpu.make_async_remote_copy(
            src_ref=stage.at[pl.ds(pl.multiple_of(target * part, part), part), cols(h)],
            dst_ref=out_ref.at[:, out_cols(seq, h)],
            send_sem=z_send.at[step - 1, h],
            recv_sem=z_recv.at[step - 1, h],
            device_id=(rep, span, target, core),
            device_id_type=MESH,
        )

    def to_self(h):
        return pltpu.make_async_copy(
            stage.at[pl.ds(pl.multiple_of(seq * part, part), part), cols(h)],
            out_ref.at[:, out_cols(seq, h)],
            own_sem.at[h],
        )

    def spread(h):
        for step in range(1, seq_count):
            to_seq(h, step).start()
        to_self(h).start()

    def launch(n, carry):
        for copy in to_partner(head_of(n)):
            copy.start()
        return carry

    shift = scalars_ref[0]
    higher = scalars_ref[1]
    rate = jnp.float32(RATE)

    def choose(first, second):
        picked = first.astype(jnp.float32) * higher + second.astype(jnp.float32) * (1.0 - higher)
        return picked.astype(jnp.bfloat16)

    def launch_across(j, carry):
        b = j + jobs
        pay_ref[:, cols(j)] = choose(q_ref[:, cols(b)], k_ref[:, cols(j)])
        pay_ref[:, cols(b)] = choose(q_ref[:, cols(j)], v_ref[:, cols(j)])
        for copy in to_across(j):
            copy.start()
        return carry

    lax.fori_loop(0, heads, launch, 0)
    lax.fori_loop(0, jobs, launch_across, 0)

    def attend_rows(query, key_blocks, value_blocks):
        scores = [
            lax.dot_general(
                query, key, (((1,), (1,)), ((), ())), preferred_element_type=jnp.float32
            )
            for key in key_blocks
        ]
        top = jnp.max(jnp.maximum(scores[0], scores[1]), axis=1, keepdims=True) * rate
        ones = jnp.ones((tokens, HD), jnp.bfloat16)
        total = None
        for score, value in zip(scores, value_blocks):
            weights = jnp.exp2(score * rate - top).astype(jnp.bfloat16)
            term = jnp.dot(
                weights, jnp.concatenate([value, ones], axis=1),
                preferred_element_type=jnp.float32,
            )
            total = term if total is None else total + term
        sums = total[:, HD:]
        return total[:, :HD] / sums, top + jnp.log(sums) * jnp.float32(LOG2E)

    def merge(near, near_lse, far, far_lse):
        far_lse = far_lse - shift
        top = jnp.maximum(near_lse, far_lse)
        near_part, far_part = jnp.exp2(near_lse - top), jnp.exp2(far_lse - top)
        mixed = (near * near_part + far * far_part) / (near_part + far_part)
        return mixed.astype(jnp.bfloat16)

    def step(n, carry):
        @pl.when(n < heads)
        def own_job():
            h = head_of(n)
            for copy in to_partner(h):
                copy.wait_recv()
            for t in range(tokens // ROWS):
                rows = pl.ds(t * ROWS, ROWS)
                result, lse = attend_rows(
                    q_ref[rows, cols(h)],
                    (k_ref[:, cols(h)], kp[:, cols(h)]),
                    (v_ref[:, cols(h)], vp[:, cols(h)]),
                )
                own[rows, cols(h)] = result
                own_lse[rows, cols(h)] = lse

        @pl.when(lax.rem(n, 2) == 1)
        def pass_on():
            j = n // 2
            for copy in to_across(j):
                copy.wait_recv()
            for copy in relay(j):
                copy.start()

        @pl.when(jnp.logical_and(lax.rem(n, 2) == 0, n > 0))
        def cross_job():
            j = n // 2 - 1
            b = j + jobs
            for copy in relay(j):
                copy.wait_recv()
            jq[...] = choose(q_ref[:, cols(j)], px[:, cols(j)])
            jk[0] = choose(px[:, cols(j)], k_ref[:, cols(b)])
            jk[1] = choose(pd[:, cols(j)], kp[:, cols(b)])
            jv[0] = choose(px[:, cols(b)], v_ref[:, cols(b)])
            jv[1] = choose(pd[:, cols(b)], vp[:, cols(b)])
            for t in range(tokens // ROWS):
                rows = pl.ds(t * ROWS, ROWS)
                result, lse = attend_rows(jq[rows, :], (jk[0], jk[1]), (jv[0], jv[1]))
                cross[rows, cols(j)] = result.astype(jnp.bfloat16)
                cross_lse[j, :, rows] = lse.T[:1, :]
                stage[rows, cols(j)] = merge(
                    own[rows, cols(j)], own_lse[rows, cols(j)], result, lse
                )
            for copy in give_back(j):
                copy.start()
            spread(j)

        return carry

    lax.fori_loop(0, heads + 1, step, 0)

    def complete(j, carry):
        b = j + jobs
        for copy in give_back(j):
            copy.wait_recv()
        for t in range(tokens // ROWS):
            rows = pl.ds(t * ROWS, ROWS)
            lse = jnp.broadcast_to(back_lse[j, :, rows], (HD, ROWS)).T
            stage[rows, cols(b)] = merge(
                own[rows, cols(b)], own_lse[rows, cols(b)],
                back[rows, cols(j)].astype(jnp.float32), lse,
            )
        spread(b)
        return carry

    lax.fori_loop(0, jobs, complete, 0)

    def drain(h, carry):
        for copy in to_partner(h):
            copy.wait_send()
        for hop in range(1, seq_count):
            to_seq(h, hop).wait_send()
            to_seq(h, hop).wait_recv()
        to_self(h).wait()
        return carry

    def drain_jobs(j, carry):
        for copy in to_across(j) + relay(j) + give_back(j):
            copy.wait_send()
        return carry

    lax.fori_loop(0, jobs, drain_jobs, 0)
    lax.fori_loop(0, heads, drain, 0)


def per_device_fused(queries, keys, values, span_order):
    tokens, width = queries.shape[2], queries.shape[3]
    heads = width // HD
    jobs = heads // 2
    half = jobs * HD
    seq_count = lax.axis_size("seq")
    bias_rate = 1.0 / (2.0 * span_order.shape[0])
    span = lax.axis_index("span")
    own = lookup(span_order, jnp.reshape(span, (1,)))
    other = lookup(span_order, jnp.reshape(1 - span, (1,)))
    bias = (own - other).astype(jnp.float32) * jnp.float32(bias_rate)
    higher = other <= own
    shift = jnp.where(higher, bias * jnp.float32(LOG2E), jnp.float32(1e30))
    scalars = jnp.concatenate([shift, higher.astype(jnp.float32)])
    query, key, value = (a.reshape(tokens, width) for a in (queries, keys, values))
    whole = pl.BlockSpec(memory_space=pltpu.VMEM)
    block = pltpu.VMEM((tokens, width), jnp.bfloat16)
    wide = pltpu.VMEM((tokens, width), jnp.float32)
    narrow = pltpu.VMEM((tokens, half), jnp.bfloat16)
    rows = pltpu.VMEM((jobs, 1, tokens), jnp.float32)
    both = pltpu.VMEM((2, tokens, HD), jnp.bfloat16)
    pairs = pltpu.SemaphoreType.DMA((2, heads))
    few = pltpu.SemaphoreType.DMA((2, jobs))
    lines = pltpu.SemaphoreType.DMA((seq_count - 1, heads))
    result = pl.pallas_call(
        functools.partial(fused_kernel, heads, seq_count),
        out_shape=jax.ShapeDtypeStruct((tokens // seq_count, width * seq_count), jnp.bfloat16),
        in_specs=[pl.BlockSpec(memory_space=pltpu.SMEM), whole, whole, whole],
        out_specs=whole,
        scratch_shapes=[block] * 4
        + [wide] * 2
        + [narrow, rows, narrow, rows, block]
        + [pltpu.VMEM((tokens, HD), jnp.bfloat16), both, both, block]
        + [pairs] * 2
        + [few] * 6
        + [lines] * 2
        + [pltpu.SemaphoreType.DMA((heads,))],
        compiler_params=pltpu.CompilerParams(
            collective_id=0, has_side_effects=True, vmem_limit_bytes=60 * 1024 * 1024
        ),
    )(scalars, query, key, value)
    return result.reshape(1, 1, tokens // seq_count, width * seq_count)


def per_device(queries, keys, values, span_order):
    tokens = queries.shape[2]
    seq_count = lax.axis_size("seq")
    part = tokens // seq_count
    fits = (
        lax.axis_size("span") == 2
        and lax.axis_size("head") == 2
        and tokens % ROWS == 0
        and part % 16 == 0
        and queries.shape[3] % (2 * HD) == 0
        and seq_count <= 8
    )
    run = per_device_fused if fits else per_device_general
    return run(queries, keys, values, span_order)


def solution(mesh):
    return jax.shard_map(
        per_device,
        mesh=mesh,
        in_specs=(
            P(("rep", "span"), "head", None, "seq"),
            P(("rep", "span"), "head", None, "seq"),
            P(("rep", "span"), "head", None, "seq"),
            P("rep"),
        ),
        out_specs=P(("rep", "span"), "head", "seq", None),
        check_vma=False,
    )
```

```python
import functools
import math

import jax
import jax.numpy as jnp
from jax import lax
from jax.experimental import pallas as pl
from jax.experimental.pallas import tpu as pltpu
from jax.sharding import PartitionSpec as P

HD = 128


def lookup(span_order, block_index):
    table = jnp.arange(span_order.shape[0], dtype=jnp.int32)
    return jnp.sum(
        jnp.where(block_index[:, None] == table[None, :], span_order[None, :], 0), axis=1
    )


def initial(query_heads):
    query_count = query_heads.shape[0]
    local_heads = query_heads.shape[1]
    return (
        jnp.full((local_heads, query_count), -1e30, jnp.float32),
        jnp.zeros((local_heads, query_count), jnp.float32),
        jnp.zeros((local_heads, query_count, HD), jnp.float32),
    )


def attend(running, query_heads, key_piece, value_piece, block_span, own_span, bias_rate):
    block_count = key_piece.shape[0]
    piece_rows = key_piece.shape[1]
    local_heads = key_piece.shape[2] // HD
    key_count = block_count * piece_rows
    score_scale = 1.0 / math.sqrt(HD)
    key_spans = jnp.repeat(block_span, piece_rows)
    allowed = key_spans <= own_span
    distance_bias = (own_span - key_spans).astype(jnp.float32) * jnp.float32(bias_rate)
    block_size = 1024
    block_total = key_count // block_size
    key_blocks = key_piece.reshape(block_total, block_size, local_heads, HD)
    value_blocks = value_piece.reshape(block_total, block_size, local_heads, HD)
    allow_blocks = allowed.reshape(block_total, block_size)
    bias_blocks = distance_bias.reshape(block_total, block_size)

    def advance(status, block_item):
        key_block, value_block, allow_block, bias_block = block_item
        maxima, totals, weighted = status
        scores = (
            jnp.einsum("qhd,khd->hqk", query_heads, key_block, preferred_element_type=jnp.float32)
            * score_scale
        )
        scores = scores - bias_block[None, None, :]
        scores = jnp.where(allow_block[None, None, :], scores, jnp.float32(-1e30))
        new_max = jnp.maximum(maxima, jnp.max(scores, axis=2))
        weights = jnp.where(
            allow_block[None, None, :], jnp.exp(scores - new_max[:, :, None]), 0.0
        ).astype(jnp.bfloat16)
        shrink = jnp.exp(maxima - new_max)
        totals = totals * shrink + jnp.sum(weights.astype(jnp.float32), axis=2)
        weighted = weighted * shrink[:, :, None] + jnp.einsum(
            "hqk,khd->hqd", weights, value_block, preferred_element_type=jnp.float32
        )
        return ((new_max, totals, weighted), None)

    running, unused = lax.scan(
        advance, running, (key_blocks, value_blocks, allow_blocks, bias_blocks)
    )
    return running


def finish(running):
    maxima, totals, weighted = running
    local_heads = weighted.shape[0]
    query_count = weighted.shape[1]
    output = (weighted / totals[:, :, None]).transpose(1, 0, 2)
    return output.reshape(1, 1, query_count, local_heads * HD).astype(jnp.bfloat16)


def per_device_general(queries, keys, values, span_order):
    half_rows = queries.shape[2]
    local_width = queries.shape[3]
    local_heads = local_width // HD
    halves = lax.axis_size("head")
    bias_rate = 1.0 / (2.0 * span_order.shape[0])
    own_span = lookup(span_order, jnp.reshape(lax.axis_index("span"), (1,)))[0]
    query_heads = queries.reshape(half_rows, local_heads, HD)
    pieces = (
        lax.all_gather(keys, ("span", "head"), axis=0, tiled=True),
        lax.all_gather(values, ("span", "head"), axis=0, tiled=True),
    )
    count = pieces[0].shape[0]
    block_index = jnp.arange(count, dtype=jnp.int32) // halves
    key_piece = pieces[0].reshape(count, half_rows, local_width)
    value_piece = pieces[1].reshape(count, half_rows, local_width)
    running = attend(
        initial(query_heads),
        query_heads,
        key_piece,
        value_piece,
        lookup(span_order, block_index),
        own_span,
        bias_rate,
    )
    result = finish(running)
    return lax.all_to_all(result, "seq", split_axis=2, concat_axis=3, tiled=True)


MESH = pl.DeviceIdType.MESH
ROWS = 256
LOG2E = 1.4426950408889634
RATE = LOG2E / math.sqrt(HD)


def fused_kernel(
    heads, seq_count, scalars_ref, q_ref, k_ref, v_ref, out_ref,
    kp, vp, px, pd, own, own_lse, cross, cross_lse, back, back_lse, stage, jq, jk, jv, pay_ref,
    p_send, p_recv, x_send, x_recv, d_send, d_recv, r_send, r_recv, z_send, z_recv, own_sem,
):
    rep, span = lax.axis_index("rep"), lax.axis_index("span")
    seq, core = lax.axis_index("seq"), lax.axis_index("head")
    partner = (rep, span, seq, 1 - core)
    across = (rep, 1 - span, seq, core)
    tokens, width = q_ref.shape
    part = tokens // seq_count
    jobs = heads // 2

    def along(step):
        return lax.rem(seq + step, seq_count)

    barrier = pltpu.get_barrier_semaphore()
    peers = [partner, across] + [(rep, span, along(i), core) for i in range(1, seq_count)]
    for peer in peers:
        pl.semaphore_signal(barrier, inc=1, device_id=peer, device_id_type=MESH)
    pl.semaphore_wait(barrier, len(peers))

    def cols(h):
        return pl.ds(pl.multiple_of(h * HD, HD), HD)

    def head_of(n):
        return lax.rem(n, 2) * jobs + n // 2

    def move(src, dst, send, recv, which, h, column, device):
        return pltpu.make_async_remote_copy(
            src_ref=src.at[:, cols(column)],
            dst_ref=dst.at[:, cols(column)],
            send_sem=send.at[which, h],
            recv_sem=recv.at[which, h],
            device_id=device,
            device_id_type=MESH,
        )

    def to_partner(h):
        return (
            move(k_ref, kp, p_send, p_recv, 0, h, h, partner),
            move(v_ref, vp, p_send, p_recv, 1, h, h, partner),
        )

    def to_across(j):
        return (
            move(pay_ref, px, x_send, x_recv, 0, j, j, across),
            move(pay_ref, px, x_send, x_recv, 1, j, j + jobs, across),
        )

    def relay(j):
        return (
            move(px, pd, d_send, d_recv, 0, j, j, partner),
            move(px, pd, d_send, d_recv, 1, j, j + jobs, partner),
        )

    def give_back(j):
        return (
            move(cross, back, r_send, r_recv, 0, j, j, across),
            pltpu.make_async_remote_copy(
                src_ref=cross_lse.at[j],
                dst_ref=back_lse.at[j],
                send_sem=r_send.at[1, j],
                recv_sem=r_recv.at[1, j],
                device_id=across,
                device_id_type=MESH,
            ),
        )

    def out_cols(from_seq, h):
        return pl.ds(pl.multiple_of(from_seq * width + h * HD, HD), HD)

    def to_seq(h, step):
        target = along(step)
        return pltpu.make_async_remote_copy(
            src_ref=stage.at[pl.ds(pl.multiple_of(target * part, part), part), cols(h)],
            dst_ref=out_ref.at[:, out_cols(seq, h)],
            send_sem=z_send.at[step - 1, h],
            recv_sem=z_recv.at[step - 1, h],
            device_id=(rep, span, target, core),
            device_id_type=MESH,
        )

    def to_self(h):
        return pltpu.make_async_copy(
            stage.at[pl.ds(pl.multiple_of(seq * part, part), part), cols(h)],
            out_ref.at[:, out_cols(seq, h)],
            own_sem.at[h],
        )

    def spread(h):
        for step in range(1, seq_count):
            to_seq(h, step).start()
        to_self(h).start()

    def launch(n, carry):
        for copy in to_partner(head_of(n)):
            copy.start()
        return carry

    shift = scalars_ref[0]
    higher = scalars_ref[1]
    rate = jnp.float32(RATE)

    def choose(first, second):
        picked = first.astype(jnp.float32) * higher + second.astype(jnp.float32) * (1.0 - higher)
        return picked.astype(jnp.bfloat16)

    def launch_across(j, carry):
        b = j + jobs
        pay_ref[:, cols(j)] = choose(q_ref[:, cols(b)], k_ref[:, cols(j)])
        pay_ref[:, cols(b)] = choose(q_ref[:, cols(j)], v_ref[:, cols(j)])
        for copy in to_across(j):
            copy.start()
        return carry

    lax.fori_loop(0, heads, launch, 0)
    lax.fori_loop(0, jobs, launch_across, 0)

    def attend_rows(query, key_blocks, value_blocks):
        scores = [
            lax.dot_general(
                query, key, (((1,), (1,)), ((), ())), preferred_element_type=jnp.float32
            )
            for key in key_blocks
        ]
        top = jnp.max(jnp.maximum(scores[0], scores[1]), axis=1, keepdims=True) * rate
        ones = jnp.ones((tokens, HD), jnp.bfloat16)
        total = None
        for score, value in zip(scores, value_blocks):
            weights = jnp.exp2(score * rate - top).astype(jnp.bfloat16)
            term = jnp.dot(
                weights, jnp.concatenate([value, ones], axis=1),
                preferred_element_type=jnp.float32,
            )
            total = term if total is None else total + term
        sums = total[:, HD:]
        return total[:, :HD] / sums, top + jnp.log(sums) * jnp.float32(LOG2E)

    def merge(near, near_lse, far, far_lse):
        far_lse = far_lse - shift
        top = jnp.maximum(near_lse, far_lse)
        near_part, far_part = jnp.exp2(near_lse - top), jnp.exp2(far_lse - top)
        mixed = (near * near_part + far * far_part) / (near_part + far_part)
        return mixed.astype(jnp.bfloat16)

    def step(n, carry):
        @pl.when(n < heads)
        def own_job():
            h = head_of(n)
            for copy in to_partner(h):
                copy.wait_recv()
            for t in range(tokens // ROWS):
                rows = pl.ds(t * ROWS, ROWS)
                result, lse = attend_rows(
                    q_ref[rows, cols(h)],
                    (k_ref[:, cols(h)], kp[:, cols(h)]),
                    (v_ref[:, cols(h)], vp[:, cols(h)]),
                )
                own[rows, cols(h)] = result
                own_lse[rows, cols(h)] = lse

        @pl.when(lax.rem(n, 2) == 1)
        def pass_on():
            j = n // 2
            for copy in to_across(j):
                copy.wait_recv()
            for copy in relay(j):
                copy.start()

        @pl.when(jnp.logical_and(lax.rem(n, 2) == 0, n > 0))
        def cross_job():
            j = n // 2 - 1
            b = j + jobs
            for copy in relay(j):
                copy.wait_recv()
            jq[...] = choose(q_ref[:, cols(j)], px[:, cols(j)])
            jk[0] = choose(px[:, cols(j)], k_ref[:, cols(b)])
            jk[1] = choose(pd[:, cols(j)], kp[:, cols(b)])
            jv[0] = choose(px[:, cols(b)], v_ref[:, cols(b)])
            jv[1] = choose(pd[:, cols(b)], vp[:, cols(b)])
            for t in range(tokens // ROWS):
                rows = pl.ds(t * ROWS, ROWS)
                result, lse = attend_rows(jq[rows, :], (jk[0], jk[1]), (jv[0], jv[1]))
                cross[rows, cols(j)] = result.astype(jnp.bfloat16)
                cross_lse[j, :, rows] = lse.T[:1, :]
                stage[rows, cols(j)] = merge(
                    own[rows, cols(j)], own_lse[rows, cols(j)], result, lse
                )
            for copy in give_back(j):
                copy.start()
            spread(j)

        return carry

    lax.fori_loop(0, heads + 1, step, 0)

    def complete(j, carry):
        b = j + jobs
        for copy in give_back(j):
            copy.wait_recv()
        for t in range(tokens // ROWS):
            rows = pl.ds(t * ROWS, ROWS)
            lse = jnp.broadcast_to(back_lse[j, :, rows], (HD, ROWS)).T
            stage[rows, cols(b)] = merge(
                own[rows, cols(b)], own_lse[rows, cols(b)],
                back[rows, cols(j)].astype(jnp.float32), lse,
            )
        spread(b)
        return carry

    lax.fori_loop(0, jobs, complete, 0)

    def drain(h, carry):
        for copy in to_partner(h):
            copy.wait_send()
        for hop in range(1, seq_count):
            to_seq(h, hop).wait_send()
            to_seq(h, hop).wait_recv()
        to_self(h).wait()
        return carry

    def drain_jobs(j, carry):
        for copy in to_across(j) + relay(j) + give_back(j):
            copy.wait_send()
        return carry

    lax.fori_loop(0, jobs, drain_jobs, 0)
    lax.fori_loop(0, heads, drain, 0)


def per_device_fused(queries, keys, values, span_order):
    tokens, width = queries.shape[2], queries.shape[3]
    heads = width // HD
    jobs = heads // 2
    half = jobs * HD
    seq_count = lax.axis_size("seq")
    bias_rate = 1.0 / (2.0 * span_order.shape[0])
    span = lax.axis_index("span")
    own = lookup(span_order, jnp.reshape(span, (1,)))
    other = lookup(span_order, jnp.reshape(1 - span, (1,)))
    bias = (own - other).astype(jnp.float32) * jnp.float32(bias_rate)
    higher = other <= own
    shift = jnp.where(higher, bias * jnp.float32(LOG2E), jnp.float32(1e30))
    scalars = jnp.concatenate([shift, higher.astype(jnp.float32)])
    query, key, value = (a.reshape(tokens, width) for a in (queries, keys, values))
    whole = pl.BlockSpec(memory_space=pltpu.VMEM)
    block = pltpu.VMEM((tokens, width), jnp.bfloat16)
    wide = pltpu.VMEM((tokens, width), jnp.float32)
    narrow = pltpu.VMEM((tokens, half), jnp.bfloat16)
    rows = pltpu.VMEM((jobs, 1, tokens), jnp.float32)
    both = pltpu.VMEM((2, tokens, HD), jnp.bfloat16)
    pairs = pltpu.SemaphoreType.DMA((2, heads))
    few = pltpu.SemaphoreType.DMA((2, jobs))
    lines = pltpu.SemaphoreType.DMA((seq_count - 1, heads))
    result = pl.pallas_call(
        functools.partial(fused_kernel, heads, seq_count),
        out_shape=jax.ShapeDtypeStruct((tokens // seq_count, width * seq_count), jnp.bfloat16),
        in_specs=[pl.BlockSpec(memory_space=pltpu.SMEM), whole, whole, whole],
        out_specs=pl.BlockSpec(memory_space=pl.ANY),
        scratch_shapes=[block] * 4
        + [wide] * 2
        + [narrow, rows, narrow, rows, block]
        + [pltpu.VMEM((tokens, HD), jnp.bfloat16), both, both, block]
        + [pairs] * 2
        + [few] * 6
        + [lines] * 2
        + [pltpu.SemaphoreType.DMA((heads,))],
        compiler_params=pltpu.CompilerParams(
            collective_id=0, has_side_effects=True, vmem_limit_bytes=60 * 1024 * 1024
        ),
    )(scalars, query, key, value)
    return result.reshape(1, 1, tokens // seq_count, width * seq_count)


def per_device(queries, keys, values, span_order):
    tokens = queries.shape[2]
    seq_count = lax.axis_size("seq")
    part = tokens // seq_count
    fits = (
        lax.axis_size("span") == 2
        and lax.axis_size("head") == 2
        and tokens % ROWS == 0
        and part % 16 == 0
        and queries.shape[3] % (2 * HD) == 0
        and seq_count <= 8
    )
    run = per_device_fused if fits else per_device_general
    return run(queries, keys, values, span_order)


def solution(mesh):
    return jax.shard_map(
        per_device,
        mesh=mesh,
        in_specs=(
            P(("rep", "span"), "head", None, "seq"),
            P(("rep", "span"), "head", None, "seq"),
            P(("rep", "span"), "head", None, "seq"),
            P("rep"),
        ),
        out_specs=P(("rep", "span"), "head", "seq", None),
        check_vma=False,
    )
```
